768 devices in a mesh: sub: 96 (over y, z), blk: 8 (over x, core).
Axes of the slice: x: 4, y: 8, z: 12, core: 2. Of those that a mesh axis runs over, the one named last changes fastest.
Arguments:
- loads: float32 [12288, 640], P(('sub', 'blk')), may hold values from -6 to 6
- schur: float32 [491520, 640], P(('sub', 'blk'))
- local_inverse: float32 [491520, 640], P(('sub', 'blk'))
- coarse_basis: float32 [6144, 640], P(('sub', 'blk')), may hold values from -2 to 2
- coarse_rows: float32 [6144, 6144], P(('sub', 'blk')), may hold values from -0.0078125 to 0.0078125
- partner: int32 [768, 3], P(('sub', 'blk')), may hold values from 0 to 7, as said below
- face_offset: int32 [768, 3], P(('sub', 'blk')), may hold values from 0 to 127, as said below
- face_length: int32 [768, 3], P(('sub', 'blk')), may hold values from 1 to 128, as said below
- coarse_index: int32 [768, 8], P(('sub', 'blk')), may hold values from 0 to 6143
Outputs:
- solution_field: float32 [12288, 640], P(('sub', 'blk'))
- residual: float32 [12288, 640], P(('sub', 'blk'))
The draws below stay inside these ranges and needn't reach their ends.
Inputs may be any that keep to these rules, and one draw needn't show every extreme that they name: In each colour the subdomains of one sub index are paired: partner names a blk index other than the subdomain's own, the pairing is symmetric, and one subdomain's 3 partners all differ. `face_length`: paired subdomains have equal lengths in that colour; in every colour of every sub index one pair has length 128 and at least one pair has length 1. face_offset + face_length <= 128.
All inputs are finite; a program needn't handle non-finite values.
Results may differ from the reference program's by a relative error of at most 0.0001.
Values sent between devices are 32-bit elements; how exact they have to be, the bound alone decides.
No kernel may reach another device: no remote copies, remote signals or barrier semaphores. Data moves between devices by JAX's collectives and lax.ppermute only.
A program may use at most 32 MiB of HBM per device.

```python
import math
import jax
import jax.numpy as jnp
from jax import lax

FACE = 128
CAP = 128
COLOURS = 3
ORDER = 640
LOADS = 16
CONSTRAINTS = 8
ITERS = 2
SUBS = 768
NCOARSE = 6144
N_SUB = 96
N_BLK = 8


def diagonal_block(key, salt):
    noise_key = jax.random.fold_in(key, salt)
    noise = jax.random.normal(noise_key, (SUBS, ORDER, ORDER), jnp.float32)
    block = noise * (0.4 / math.sqrt(ORDER)) + jnp.eye(ORDER, dtype=jnp.float32)[None]
    return block.reshape(SUBS * ORDER, ORDER)


def draw_schur(key, part):
    return diagonal_block(key, 101)


def draw_local_inverse(key, part):
    return diagonal_block(key, 202)


def matching(key):
    base = jax.random.fold_in(key, 17)
    label_key = jax.random.fold_in(base, 1)
    round_key = jax.random.fold_in(base, 2)
    length_key = jax.random.fold_in(base, 3)
    labels = jax.vmap(lambda k: jax.random.permutation(k, N_BLK))(jax.random.split(label_key, N_SUB)).astype(jnp.int32)
    rounds = jax.vmap(lambda k: jax.random.permutation(k, N_BLK - 1)[:COLOURS])(jax.random.split(round_key, N_SUB)).astype(jnp.int32)
    owner = jnp.argsort(labels, axis=1).astype(jnp.int32)
    last = N_BLK - 1
    mine = labels[:, :, None]
    chosen = rounds[:, None, :]
    other = jnp.where(mine == last, chosen, jnp.where(mine == chosen, last, (2 * chosen - mine) % last))
    partner = jnp.take_along_axis(owner, other.reshape(N_SUB, N_BLK * COLOURS), axis=1).reshape(N_SUB, N_BLK, COLOURS)
    table = jax.random.randint(length_key, (N_SUB, N_BLK, COLOURS), 1, CAP + 1, dtype=jnp.int32)
    table = table.at[:, 0, :].set(CAP)
    table = table.at[:, 1, :].set(1)
    table = table.at[:, 2, :].set(1)
    pair_key = jnp.minimum(mine, other)
    length = jnp.take_along_axis(table, pair_key, axis=1)
    return (partner.reshape(SUBS, COLOURS).astype(jnp.int32), length.reshape(SUBS, COLOURS).astype(jnp.int32))


def draw_partner(key, part):
    return matching(key)[0]


def draw_face_length(key, part):
    return matching(key)[1]


def draw_face_offset(key, part):
    length = matching(key)[1]
    offset_key = jax.random.fold_in(key, 29)
    drawn = jax.random.randint(offset_key, (SUBS, COLOURS), 0, CAP - length + 1, dtype=jnp.int32)
    return jnp.where(length == 1, CAP - 1, drawn).astype(jnp.int32)


def touch_ends(entries, stream_key, low, top_value):
    extent = entries.shape
    index_at = [jax.random.randint(jax.random.fold_in(stream_key, axis), (), 0, extent[axis]) for axis in range(len(extent))]
    entries = entries.at[tuple(index_at)].set(low)
    longest = extent.index(max(extent))
    index_at[longest] = (index_at[longest] + 1) % extent[longest]
    return entries.at[tuple(index_at)].set(top_value)


def levels(own_key, dims, shards, least, high):
    gain, own = 1.0, jax.random.fold_in(own_key, 6)
    for dim, blocks in shards:
        heights = jnp.exp(jax.random.uniform(jax.random.fold_in(own, dim), (blocks,), jnp.float32, least / len(shards), high / len(shards)))
        gain = gain * jnp.repeat(heights, dims[dim] // blocks).reshape([-1 if axis == dim else 1 for axis in range(len(dims))])
    return gain


def bell_draw(key, shape, scale, reach, cuts=(), kind=jnp.bfloat16):
    array = jax.random.normal(key, shape, jnp.float32) * scale
    if len(cuts) > 0:
        array = levels(key, shape, cuts, -0.22, 0.18) * array
    return jnp.clip(array, min=-reach, max=reach).astype(kind)


def setup_inputs(seed: int = 0) -> dict:
    arg_keys = jax.random.split(jax.random.key(seed), 10)
    return {
        "loads": bell_draw(arg_keys[0], (SUBS * LOADS, ORDER), 1.0, 6.0, ((0, 768),), jnp.float32),
        "schur": draw_schur(jax.random.fold_in(arg_keys[9], 71), 0),
        "local_inverse": draw_local_inverse(jax.random.fold_in(arg_keys[9], 71), 0),
        "coarse_basis": bell_draw(arg_keys[3], (SUBS * CONSTRAINTS, ORDER), CONSTRAINTS ** -0.5, 2.0, ((0, 768),), jnp.float32),
        "coarse_rows": bell_draw(arg_keys[4], (NCOARSE, NCOARSE), (NCOARSE * ORDER // CONSTRAINTS) ** -0.5, 0.0078125, ((0, 768),), jnp.float32),
        "partner": draw_partner(jax.random.fold_in(arg_keys[9], 71), 0),
        "face_offset": draw_face_offset(jax.random.fold_in(arg_keys[9], 71), 0),
        "face_length": draw_face_length(jax.random.fold_in(arg_keys[9], 71), 0),
        "coarse_index": touch_ends(jax.random.randint(arg_keys[8], (SUBS, CONSTRAINTS), 0, NCOARSE), jax.random.fold_in(arg_keys[8], 1), 0, NCOARSE - 1).astype(jnp.int32),
    }


highest = lax.Precision.HIGHEST
low_bound = 0.5
high_bound = 4.0


def assemble(values, partner, face_offset, face_length):
    lower = values[:, :, :FACE]
    upper = values[:, :, FACE:2 * FACE]
    zero_rim = jnp.zeros((N_BLK,) + lower.shape[1:], values.dtype)
    lower_new = lower + jnp.concatenate([zero_rim, upper[:-N_BLK]], 0)
    upper_new = upper + jnp.concatenate([lower[N_BLK:], zero_rim], 0)
    positions = jnp.arange(CAP, dtype=jnp.int32)[None, :]
    group = (jnp.arange(SUBS, dtype=jnp.int32) // N_BLK) * N_BLK
    pieces = [lower_new, upper_new]
    for colour in range(COLOURS):
        region = values[:, :, 2 * FACE + colour * CAP:2 * FACE + (colour + 1) * CAP]
        begin = face_offset[:, colour][:, None]
        count = face_length[:, colour][:, None]
        source = jnp.broadcast_to(((positions + begin) % CAP)[:, None, :], region.shape)
        outgoing = jnp.take_along_axis(region, source, axis=2)
        outgoing = jnp.where((positions < count)[:, None, :], outgoing, 0.0)
        incoming = outgoing[(group + partner[:, colour]).astype(jnp.int32)]
        back = jnp.broadcast_to(((positions - begin) % CAP)[:, None, :], region.shape)
        placed = jnp.take_along_axis(incoming, back, axis=2)
        inside = (positions >= begin) & (positions < begin + count)
        pieces.append(region + jnp.where(inside[:, None, :], placed, 0.0))
    return jnp.concatenate(pieces, axis=2)


def weights(face_offset, face_length):
    sub_of = jnp.arange(SUBS, dtype=jnp.int32) // N_BLK
    lower = jnp.where(sub_of > 0, 0.5, 1.0)[:, None] * jnp.ones((1, FACE), jnp.float32)
    upper = jnp.where(sub_of < N_SUB - 1, 0.5, 1.0)[:, None] * jnp.ones((1, FACE), jnp.float32)
    positions = jnp.arange(CAP, dtype=jnp.int32)[None, :]
    pieces = [lower, upper]
    for colour in range(COLOURS):
        begin = face_offset[:, colour][:, None]
        inside = (positions >= begin) & (positions < begin + face_length[:, colour][:, None])
        pieces.append(jnp.where(inside, 0.5, 1.0))
    return jnp.concatenate(pieces, axis=1)[:, None, :]


def reference(loads, schur, local_inverse, coarse_basis, coarse_rows, partner, face_offset, face_length, coarse_index):
    residual = loads.reshape(SUBS, LOADS, ORDER)
    schur_all = schur.reshape(SUBS, ORDER, ORDER)
    inverse_all = local_inverse.reshape(SUBS, ORDER, ORDER)
    basis = coarse_basis.reshape(SUBS, CONSTRAINTS, ORDER)
    weight = weights(face_offset, face_length)

    def precondition(values):
        scaled = weight * assemble(values, partner, face_offset, face_length)
        constraint = jnp.einsum('dlm,dcm->dlc', scaled, basis, precision=highest)
        flat = jnp.transpose(constraint, (0, 2, 1)).reshape(SUBS * CONSTRAINTS, LOADS)
        summed = jax.ops.segment_sum(flat, coarse_index.reshape(-1).astype(jnp.int32), num_segments=NCOARSE)
        coarse = jnp.dot(coarse_rows, summed, precision=highest, preferred_element_type=jnp.float32)
        coarse = jnp.transpose(coarse.reshape(SUBS, CONSTRAINTS, LOADS), (0, 2, 1))
        local = jnp.einsum('dlm,dmn->dln', scaled, inverse_all, precision=highest)
        local = local + jnp.einsum('dlc,dcm->dlm', coarse, basis, precision=highest)
        return assemble(weight * local, partner, face_offset, face_length)

    def apply(values):
        return jnp.einsum('dlm,dmn->dln', values, schur_all, precision=highest)

    theta = (high_bound + low_bound) / 2.0
    delta = (high_bound - low_bound) / 2.0
    sigma = theta / delta
    rho = 1.0 / sigma
    step = precondition(residual) / theta
    solution = step
    residual = residual - apply(step)
    for index in range(1, ITERS):
        rho_next = 1.0 / (2.0 * sigma - rho)
        step = (rho_next * rho) * step + (2.0 * rho_next / delta) * precondition(residual)
        rho = rho_next
        solution = solution + step
        residual = residual - apply(step)
    return solution.reshape(SUBS * LOADS, ORDER), residual.reshape(SUBS * LOADS, ORDER)
```

```python
import functools

import jax
import jax.numpy as jnp
from jax import lax
from jax.experimental import pallas as pl
from jax.experimental.pallas import tpu as pltpu
from jax.sharding import Mesh
from jax.sharding import PartitionSpec as P

FACE = 128
COLOURS = 3
ORDER = 640
LOADS = 16
CONS = 8
NY, NZ, NX, NC = 8, 12, 4, 2
PEERS = NX * NC
GROUP = NY * NX
CHUNKS = 48
SUB = ("y", "z")
BLK = ("x", "c")
ALL = ("y", "z", "x", "c")

highest = lax.Precision.HIGHEST
LOW, HIGH = 0.5, 4.0
THETA = (HIGH + LOW) / 2.0
DELTA = (HIGH - LOW) / 2.0
SIGMA = THETA / DELTA
RHO0 = 1.0 / SIGMA
RHO1 = 1.0 / (2.0 * SIGMA - RHO0)

VM = pl.BlockSpec(memory_space=pltpu.VMEM)
SM = pl.BlockSpec(memory_space=pltpu.SMEM)


def f32(*shape):
    return jax.ShapeDtypeStruct(shape, jnp.float32)


def call(body, ins, outs, name):
    return pl.pallas_call(
        body,
        in_specs=ins,
        out_specs=[VM] * len(outs),
        out_shape=outs,
        name=name,
    )


def lanes(rows=LOADS):
    return lax.broadcasted_iota(jnp.int32, (rows, FACE), 1)


def region(colour):
    return slice((2 + colour) * FACE, (3 + colour) * FACE)


def pack(pieces, partner, offset, length, buf, low, up):
    low[...] = pieces[0]
    up[...] = pieces[1]
    buf[...] = jnp.zeros(buf.shape, jnp.float32)
    for k in range(COLOURS):
        turn = (FACE - offset[0, k]) % FACE
        rolled = pltpu.roll(pieces[2 + k], turn, 1)
        out = jnp.where(lanes() < length[0, k], rolled, 0.0)
        buf[pl.ds(pl.multiple_of(partner[0, k] * LOADS, LOADS), LOADS), :] = out


def inside(offset, length, k):
    at = lanes()
    return (at >= offset[0, k]) & (at < offset[0, k] + length[0, k])


def weights(offset, length):
    sub = lax.axis_index("y") * NZ + lax.axis_index("z")
    parts = [
        jnp.where(sub > 0, 0.5, 1.0),
        jnp.where(sub < NY * NZ - 1, 0.5, 1.0),
    ]
    for k in range(COLOURS):
        parts.append(jnp.where(inside(offset, length, k), 0.5, 1.0))
    return parts


def assembled(values, recv, below, above, partner, offset, length):
    parts = [values[:, :FACE] + below[...], values[:, FACE : 2 * FACE] + above[...]]
    for k in range(COLOURS):
        got = recv[pl.ds(pl.multiple_of(partner[0, k] * LOADS, LOADS), LOADS), :]
        turned = pltpu.roll(got, offset[0, k], 1)
        parts.append(
            values[:, region(k)] + jnp.where(inside(offset, length, k), turned, 0.0)
        )
    return parts


def pack_body(values, partner, offset, length, buf, low, up):
    pieces = [values[:, i * FACE : (i + 1) * FACE] for i in range(5)]
    pack(pieces, partner, offset, length, buf, low, up)


def constraint_row(a, basis):
    tiled = jnp.concatenate([a] * CONS, axis=0)
    prod = lax.dot_general(
        basis[...],
        tiled,
        (((1,), (1,)), ((), ())),
        precision=highest,
        preferred_element_type=jnp.float32,
    )
    row = lax.broadcasted_iota(jnp.int32, (CONS, FACE), 0)
    own = lanes(CONS) // LOADS == row
    return jnp.sum(jnp.where(own, prod, 0.0), axis=0, keepdims=True)


def scaled_body(first, *refs):
    if first:
        values, recv, below, above, partner, offset, length, basis, index, a_out, msg = refs
    else:
        values, recv, below, above, partner, offset, length, basis, a_out, msg = refs
    parts = assembled(values, recv, below, above, partner, offset, length)
    parts = [w * p for w, p in zip(weights(offset, length), parts)]
    a = jnp.concatenate(parts, axis=1)
    a_out[...] = a
    row = jnp.broadcast_to(constraint_row(a, basis), (8, FACE))
    if first:
        place = (lax.axis_index("y") * NX + lax.axis_index("x")) % 16
        at = lanes(8)
        marks = jnp.zeros((8, FACE), jnp.float32)
        for j in range(CONS):
            marks = jnp.where(at == place * CONS + j, index[0, j].astype(jnp.float32), marks)
        odd = lax.broadcasted_iota(jnp.int32, (8, FACE), 0) % 2 == 1
        row = jnp.where(odd, marks, row)
    for t in range(msg.shape[0] // 8):
        msg[8 * t : 8 * t + 8, :] = row


def spread_body(first, got, out):
    if first:
        cons = got[pl.ds(0, GROUP, 2), :]
        marks = got[pl.ds(1, GROUP, 2), :]
        halves = [jnp.sum(marks[16 * q : 16 * q + 16], axis=0, keepdims=True) for q in range(2)]
        tail = jnp.concatenate(halves + [jnp.zeros((6, FACE), jnp.float32)], axis=0)
        block = jnp.concatenate([cons, tail], axis=0)
    else:
        block = got[...]
    rows = block.shape[0]
    for z in range(NZ):
        out[z * rows : (z + 1) * rows, :] = block


def lane_take(x, idx):
    return jnp.take_along_axis(x, idx, axis=1, mode="promise_in_bounds")


def select_into(own, other, rows, sel):
    def step(z, carry):
        for half, src in enumerate((own, other)):
            for q in range(2):
                want = src[pl.ds(z * 40 + 32 + q, 1), :].astype(jnp.int32)
                want = jnp.broadcast_to(want, (8, FACE))
                high = want // FACE
                low = want % FACE
                acc = jnp.zeros((8, FACE), jnp.float32)
                for ch in range(CHUNKS):
                    part = lane_take(rows[:, ch * FACE : (ch + 1) * FACE], low)
                    acc = jnp.where(high == ch, part, acc)
                to = ((half * NZ + z) * 2 + q) * 8
                sel[pl.ds(pl.multiple_of(to, 8), 8), :] = acc
        return carry

    lax.fori_loop(0, NZ, step, 0)


def coarse_part(own, other, sel, pitch):
    group = lanes(8) // LOADS

    def step(z, accs):
        accs = list(accs)
        for half, src in enumerate((own, other)):
            for q in range(2):
                at = ((half * NZ + z) * 2 + q) * 8
                block = sel[pl.ds(pl.multiple_of(at, 8), 8), :]
                vals = src[pl.ds(pl.multiple_of(z * pitch + 16 * q, 8), 16), :]
                for p in range(16):
                    wide = lane_take(block, group + p * CONS)
                    accs[p % 4] = accs[p % 4] + wide * vals[p : p + 1, :]
        return tuple(accs)

    zero = jnp.zeros((8, FACE), jnp.float32)
    accs = lax.fori_loop(0, NZ, step, (zero,) * 4)
    acc = (accs[0] + accs[1]) + (accs[2] + accs[3])
    fold = lax.broadcasted_iota(jnp.int32, (LOADS, FACE), 0) == lanes() % LOADS
    return lax.dot_general(
        jnp.where(fold, 1.0, 0.0),
        acc,
        (((1,), (1,)), ((), ())),
        precision=highest,
        preferred_element_type=jnp.float32,
    )


def local_body(first, *refs):
    if first:
        own, other, rows, local, basis, partner, offset, length, w_out, buf, low, up, sel = refs
        select_into(own, other, rows, sel)
        pitch = 40
    else:
        own, other, sel, local, basis, partner, offset, length, w_out, buf, low, up = refs
        pitch = 32
    coarse = coarse_part(own, other, sel, pitch)
    full = local[...] + jnp.dot(
        coarse, basis[...], precision=highest, preferred_element_type=jnp.float32
    )
    scale = weights(offset, length)
    parts = [scale[i] * full[:, i * FACE : (i + 1) * FACE] for i in range(5)]
    w_out[...] = jnp.concatenate(parts, axis=1)
    pack(parts, partner, offset, length, buf, low, up)


def step_body(first, *refs):
    if first:
        values, recv, below, above, partner, offset, length, step = refs
        parts = assembled(values, recv, below, above, partner, offset, length)
        step[...] = jnp.concatenate(parts, axis=1) / THETA
    else:
        values, recv, below, above, partner, offset, length, prev, step, total = refs
        parts = assembled(values, recv, below, above, partner, offset, length)
        new = (RHO1 * RHO0) * prev[...] + (2.0 * RHO1 / DELTA) * jnp.concatenate(parts, axis=1)
        step[...] = new
        total[...] = prev[...] + new


def product(left, right):
    return jnp.dot(left, right, precision=highest, preferred_element_type=jnp.float32)


def per_device(
    loads, schur, local_inverse, coarse_basis, coarse_rows, partner, offset, length, index
):
    faces = (partner, offset, length)
    ends = NY * NZ - 1
    up_pairs = [(i, i + 1) for i in range(ends)]
    down_pairs = [(i + 1, i) for i in range(ends)]
    packed_outs = [f32(PEERS * LOADS, FACE), f32(LOADS, FACE), f32(LOADS, FACE)]

    def exchange(buf, low, up):
        recv = lax.all_to_all(
            buf.reshape(PEERS, LOADS, FACE), BLK, split_axis=0, concat_axis=0, tiled=True
        )
        below = lax.ppermute(up, SUB, up_pairs)
        above = lax.ppermute(low, SUB, down_pairs)
        return recv.reshape(PEERS * LOADS, FACE), below, above

    def precondition(residual, first, sel):
        packed = call(pack_body, [VM, SM, SM, SM], packed_outs, "pack")(residual, *faces)
        recv, below, above = exchange(*packed)
        per = 2 if first else 1
        ins = [VM, VM, VM, VM, SM, SM, SM, VM] + ([SM] if first else [])
        extra = (index,) if first else ()
        a, msg = call(
            functools.partial(scaled_body, first),
            ins,
            [f32(LOADS, ORDER), f32(GROUP * per, FACE)],
            "scaled",
        )(residual, recv, below, above, *faces, coarse_basis, *extra)
        got = lax.all_to_all(
            msg.reshape(GROUP, per, FACE), ("y", "x"), split_axis=0, concat_axis=0, tiled=True
        )
        pitch = 40 if first else 32
        (wide,) = call(
            functools.partial(spread_body, first), [VM], [f32(NZ * pitch, FACE)], "spread"
        )(got.reshape(GROUP * per, FACE))
        own = lax.all_to_all(
            wide.reshape(NZ, pitch, FACE), "z", split_axis=0, concat_axis=0, tiled=True
        ).reshape(NZ * pitch, FACE)
        other = lax.ppermute(own, "c", [(0, 1), (1, 0)])
        local = product(a, local_inverse)
        outs = [f32(LOADS, ORDER)] + packed_outs
        third = coarse_rows if first else sel
        if first:
            outs = outs + [f32(CHUNKS * 8, FACE)]
        res = call(
            functools.partial(local_body, first),
            [VM, VM, VM, VM, VM, SM, SM, SM],
            outs,
            "local",
        )(own, other, third, local, coarse_basis, *faces)
        if first:
            sel = res[4]
        recv, below, above = exchange(*res[1:4])
        return (res[0], recv, below, above), sel

    base = [VM, VM, VM, VM, SM, SM, SM]
    done, sel = precondition(loads, True, None)
    (step,) = call(functools.partial(step_body, True), base, [f32(LOADS, ORDER)], "step")(
        *done, *faces
    )
    residual = loads - product(step, schur)
    done, sel = precondition(residual, False, sel)
    step, total = call(
        functools.partial(step_body, False), base + [VM], [f32(LOADS, ORDER)] * 2, "step"
    )(*done, *faces, step)
    residual = residual - product(step, schur)
    return (total, residual)


def solution(mesh):
    finer = Mesh(mesh.devices.reshape(NY, NZ, NX, NC), ALL)
    spec = P(ALL, None)
    return jax.shard_map(
        per_device, mesh=finer, in_specs=(spec,) * 9, out_specs=(spec, spec), check_vma=False
    )
```

```python
import functools

import jax
import jax.numpy as jnp
from jax import lax
from jax.experimental import pallas as pl
from jax.experimental.pallas import tpu as pltpu
from jax.sharding import Mesh
from jax.sharding import PartitionSpec as P

FACE = 128
COLOURS = 3
ORDER = 640
LOADS = 16
CONS = 8
NY, NZ, NX, NC = 8, 12, 4, 2
PEERS = NX * NC
GROUP = NY * NX
CHUNKS = 48
SUB = ("y", "z")
BLK = ("x", "c")
ALL = ("y", "z", "x", "c")

highest = lax.Precision.HIGHEST
LOW, HIGH = 0.5, 4.0
THETA = (HIGH + LOW) / 2.0
DELTA = (HIGH - LOW) / 2.0
SIGMA = THETA / DELTA
RHO0 = 1.0 / SIGMA
RHO1 = 1.0 / (2.0 * SIGMA - RHO0)

VM = pl.BlockSpec(memory_space=pltpu.VMEM)
SM = pl.BlockSpec(memory_space=pltpu.SMEM)


class Column:
    def __init__(self, ref, start):
        self.ref, self.start = ref, start

    def __getitem__(self, at):
        return self.ref[at[0], self.start + at[1]]


def split_table(table):
    return tuple(Column(table, 3 * i) for i in range(4))


def f32(*shape):
    return pltpu.VMEM(shape, jnp.float32)


class Near:
    def __init__(self, x):
        self.x = pltpu.with_memory_space_constraint(x, pltpu.VMEM)


def near(x):
    return x.x if isinstance(x, Near) else Near(x).x


def call(body, ins, outs, name):
    run = pl.pallas_call(
        body,
        in_specs=ins,
        out_specs=[VM] * len(outs),
        out_shape=outs,
        name=name,
        compiler_params=pltpu.CompilerParams(vmem_limit_bytes=8 * 1024 * 1024),
    )

    def placed(*args):
        return run(*(near(x) if s is VM else x for s, x in zip(ins, args)))

    return placed


def lanes(rows=LOADS):
    return lax.broadcasted_iota(jnp.int32, (rows, FACE), 1)


def region(colour):
    return slice((2 + colour) * FACE, (3 + colour) * FACE)


def pack(pieces, partner, offset, length, buf, low, up):
    low[...] = pieces[0]
    up[...] = pieces[1]
    buf[...] = jnp.zeros(buf.shape, jnp.float32)
    for k in range(COLOURS):
        turn = (FACE - offset[0, k]) % FACE
        rolled = pltpu.roll(pieces[2 + k], turn, 1)
        out = jnp.where(lanes() < length[0, k], rolled, 0.0)
        buf[pl.ds(pl.multiple_of(partner[0, k] * LOADS, LOADS), LOADS), :] = out


def inside(offset, length, k):
    at = lanes()
    return (at >= offset[0, k]) & (at < offset[0, k] + length[0, k])


def weights(offset, length):
    sub = lax.axis_index("y") * NZ + lax.axis_index("z")
    parts = [
        jnp.where(sub > 0, 0.5, 1.0),
        jnp.where(sub < NY * NZ - 1, 0.5, 1.0),
    ]
    for k in range(COLOURS):
        parts.append(jnp.where(inside(offset, length, k), 0.5, 1.0))
    return parts


def assembled(values, recv, below, above, partner, offset, length):
    parts = [values[:, :FACE] + below[...], values[:, FACE : 2 * FACE] + above[...]]
    for k in range(COLOURS):
        got = recv[pl.ds(pl.multiple_of(partner[0, k] * LOADS, LOADS), LOADS), :]
        turned = pltpu.roll(got, offset[0, k], 1)
        parts.append(
            values[:, region(k)] + jnp.where(inside(offset, length, k), turned, 0.0)
        )
    return parts


def pack_body(values, partner, offset, length, buf, low, up):
    pieces = [values[:, i * FACE : (i + 1) * FACE] for i in range(5)]
    pack(pieces, partner, offset, length, buf, low, up)


def constraint_row(a, basis):
    tiled = jnp.concatenate([a] * CONS, axis=0)
    prod = lax.dot_general(
        basis[...],
        tiled,
        (((1,), (1,)), ((), ())),
        precision=highest,
        preferred_element_type=jnp.float32,
    )
    row = lax.broadcasted_iota(jnp.int32, (CONS, FACE), 0)
    own = lanes(CONS) // LOADS == row
    return jnp.sum(jnp.where(own, prod, 0.0), axis=0, keepdims=True)


def scaled_body(first, *refs):
    values, recv, below, above, table, basis, a_out, msg = refs
    partner, offset, length, index = split_table(table)
    parts = assembled(values, recv, below, above, partner, offset, length)
    parts = [w * p for w, p in zip(weights(offset, length), parts)]
    a = jnp.concatenate(parts, axis=1)
    a_out[...] = a
    row = jnp.broadcast_to(constraint_row(a, basis), (8, FACE))
    if first:
        place = (lax.axis_index("y") * NX + lax.axis_index("x")) % 16
        at = lanes(8)
        marks = jnp.zeros((8, FACE), jnp.float32)
        for j in range(CONS):
            marks = jnp.where(at == place * CONS + j, index[0, j].astype(jnp.float32), marks)
        odd = lax.broadcasted_iota(jnp.int32, (8, FACE), 0) % 2 == 1
        row = jnp.where(odd, marks, row)
    for t in range(msg.shape[0] // 8):
        msg[8 * t : 8 * t + 8, :] = row


def spread_body(first, got, out):
    if first:
        cons = got[pl.ds(0, GROUP, 2), :]
        marks = got[pl.ds(1, GROUP, 2), :]
        halves = [jnp.sum(marks[16 * q : 16 * q + 16], axis=0, keepdims=True) for q in range(2)]
        tail = jnp.concatenate(halves + [jnp.zeros((6, FACE), jnp.float32)], axis=0)
        block = jnp.concatenate([cons, tail], axis=0)
    else:
        block = got[...]
    rows = block.shape[0]
    for z in range(NZ):
        out[z * rows : (z + 1) * rows, :] = block


def lane_take(x, idx):
    return jnp.take_along_axis(x, idx, axis=1, mode="promise_in_bounds")


def select_into(own, other, rows, sel):
    def step(z, carry):
        for half, src in enumerate((own, other)):
            for q in range(2):
                want = src[pl.ds(z * 40 + 32 + q, 1), :].astype(jnp.int32)
                want = jnp.broadcast_to(want, (8, FACE))
                high = want // FACE
                low = want % FACE
                acc = jnp.zeros((8, FACE), jnp.float32)
                for ch in range(CHUNKS):
                    part = lane_take(rows[:, ch * FACE : (ch + 1) * FACE], low)
                    acc = jnp.where(high == ch, part, acc)
                to = ((half * NZ + z) * 2 + q) * 8
                sel[pl.ds(pl.multiple_of(to, 8), 8), :] = acc
        return carry

    lax.fori_loop(0, NZ, step, 0)


def coarse_part(own, other, sel, pitch):
    group = lanes(8) // LOADS

    def step(z, accs):
        accs = list(accs)
        for half, src in enumerate((own, other)):
            for q in range(2):
                at = ((half * NZ + z) * 2 + q) * 8
                block = sel[pl.ds(pl.multiple_of(at, 8), 8), :]
                vals = src[pl.ds(pl.multiple_of(z * pitch + 16 * q, 8), 16), :]
                for p in range(16):
                    wide = lane_take(block, group + p * CONS)
                    accs[p % 4] = accs[p % 4] + wide * vals[p : p + 1, :]
        return tuple(accs)

    zero = jnp.zeros((8, FACE), jnp.float32)
    accs = lax.fori_loop(0, NZ, step, (zero,) * 4)
    acc = (accs[0] + accs[1]) + (accs[2] + accs[3])
    fold = lax.broadcasted_iota(jnp.int32, (LOADS, FACE), 0) == lanes() % LOADS
    return lax.dot_general(
        jnp.where(fold, 1.0, 0.0),
        acc,
        (((1,), (1,)), ((), ())),
        precision=highest,
        preferred_element_type=jnp.float32,
    )


def local_body(first, *refs):
    if first:
        own, other, rows, local, basis, table, w_out, buf, low, up, sel = refs
        select_into(own, other, rows, sel)
        pitch = 40
    else:
        own, other, sel, local, basis, table, w_out, buf, low, up = refs
        pitch = 32
    partner, offset, length, _ = split_table(table)
    coarse = coarse_part(own, other, sel, pitch)
    full = local[...] + jnp.dot(
        coarse, basis[...], precision=highest, preferred_element_type=jnp.float32
    )
    scale = weights(offset, length)
    parts = [scale[i] * full[:, i * FACE : (i + 1) * FACE] for i in range(5)]
    w_out[...] = jnp.concatenate(parts, axis=1)
    pack(parts, partner, offset, length, buf, low, up)


def minus_product(base, step, schur):
    return base[...] - jnp.dot(
        step, schur[...], precision=highest, preferred_element_type=jnp.float32
    )


def step_body(first, *refs):
    values, recv, below, above, table, residual, schur, *rest = refs
    partner, offset, length, _ = split_table(table)
    new = jnp.concatenate(
        assembled(values, recv, below, above, partner, offset, length), axis=1
    )
    if first:
        step, left, buf, low, up = rest
        new = new / THETA
        step[...] = new
        out = minus_product(residual, new, schur)
        left[...] = out
        pack(
            [out[:, i * FACE : (i + 1) * FACE] for i in range(5)],
            partner, offset, length, buf, low, up,
        )
    else:
        prev, total, left = rest
        new = (RHO1 * RHO0) * prev[...] + (2.0 * RHO1 / DELTA) * new
        total[...] = prev[...] + new
        left[...] = minus_product(residual, new, schur)


def product(left, right):
    return jnp.dot(left, right, precision=highest, preferred_element_type=jnp.float32)


def per_device(
    loads, schur, local_inverse, coarse_basis, coarse_rows, partner, offset, length, index
):
    faces = [pltpu.with_memory_space_constraint(x, pltpu.HBM) for x in (partner, offset, length)]
    loads, schur, basis = Near(loads), Near(schur), Near(coarse_basis)
    table = jnp.concatenate([partner, offset, length, index], axis=1)
    ends = NY * NZ - 1
    up_pairs = [(i, i + 1) for i in range(ends)]
    down_pairs = [(i + 1, i) for i in range(ends)]
    packed_outs = [f32(PEERS * LOADS, FACE), f32(LOADS, FACE), f32(LOADS, FACE)]

    def exchange(buf, low, up):
        recv = lax.all_to_all(
            buf.reshape(PEERS, LOADS, FACE), BLK, split_axis=0, concat_axis=0, tiled=True
        )
        below = lax.ppermute(up, SUB, up_pairs)
        above = lax.ppermute(low, SUB, down_pairs)
        return recv.reshape(PEERS * LOADS, FACE), below, above

    def precondition(packed, residual, first, sel):
        recv, below, above = exchange(*packed)
        per = 2 if first else 1
        ins = [VM, VM, VM, VM, SM, VM]
        a, msg = call(
            functools.partial(scaled_body, first),
            ins,
            [f32(LOADS, ORDER), f32(GROUP * per, FACE)],
            "scaled",
        )(residual, recv, below, above, table, basis)
        got = lax.all_to_all(
            msg.reshape(GROUP, per, FACE), ("y", "x"), split_axis=0, concat_axis=0, tiled=True
        )
        pitch = 40 if first else 32
        (wide,) = call(
            functools.partial(spread_body, first), [VM], [f32(NZ * pitch, FACE)], "spread"
        )(got.reshape(GROUP * per, FACE))
        own = lax.all_to_all(
            wide.reshape(NZ, pitch, FACE), "z", split_axis=0, concat_axis=0, tiled=True
        ).reshape(NZ * pitch, FACE)
        other = lax.ppermute(own, "c", [(0, 1), (1, 0)])
        local = product(a, local_inverse)
        outs = [f32(LOADS, ORDER)] + packed_outs
        third = coarse_rows if first else sel
        if first:
            outs = outs + [f32(CHUNKS * 8, FACE)]
        res = call(
            functools.partial(local_body, first),
            [VM, VM, VM, VM, VM, SM],
            outs,
            "local",
        )(own, other, third, local, basis, table)
        if first:
            sel = res[4]
        recv, below, above = exchange(*res[1:4])
        return (res[0], recv, below, above), sel

    base = [VM, VM, VM, VM, SM, VM, VM]
    packed = call(pack_body, [VM, SM, SM, SM], packed_outs, "pack")(loads, *faces)
    done, sel = precondition(packed, loads, True, None)
    step, residual, *packed = call(
        functools.partial(step_body, True),
        base,
        [f32(LOADS, ORDER), f32(LOADS, ORDER)] + packed_outs,
        "step",
    )(*done, table, loads, schur)
    done, sel = precondition(packed, residual, False, sel)
    plain = jax.ShapeDtypeStruct((LOADS, ORDER), jnp.float32)
    return tuple(
        call(functools.partial(step_body, False), base + [VM], [plain, plain], "step")(
            *done, table, residual, schur, step
        )
    )


def solution(mesh):
    finer = Mesh(mesh.devices.reshape(NY, NZ, NX, NC), ALL)
    spec = P(ALL, None)
    return jax.shard_map(
        per_device, mesh=finer, in_specs=(spec,) * 9, out_specs=(spec, spec), check_vma=False
    )
```

```python
import functools

import jax
import jax.numpy as jnp
from jax import lax
from jax.experimental import pallas as pl
from jax.experimental.pallas import tpu as pltpu
from jax.sharding import Mesh
from jax.sharding import PartitionSpec as P

FACE = 128
COLOURS = 3
ORDER = 640
LOADS = 16
CONS = 8
NY, NZ, NX, NC = 8, 12, 4, 2
NV = 2
PEERS = NX * NC
GROUP = NY * NX
HALF = NZ * GROUP
CHUNKS = 48
LINE = ("u", "v")
SUB = ("y", "u", "v")
PAIR = ("v", "x", "c")
ALL = ("y", "u", "v", "x", "c")

highest = lax.Precision.HIGHEST
LOW, HIGH = 0.5, 4.0
THETA = (HIGH + LOW) / 2.0
DELTA = (HIGH - LOW) / 2.0
SIGMA = THETA / DELTA
RHO0 = 1.0 / SIGMA
RHO1 = 1.0 / (2.0 * SIGMA - RHO0)

VM = pl.BlockSpec(memory_space=pltpu.VMEM)
SM = pl.BlockSpec(memory_space=pltpu.SMEM)
LATE = pl.BlockSpec(memory_space=pltpu.VMEM)
HB = pl.BlockSpec(memory_space=pl.ANY)


class Column:
    def __init__(self, ref, start):
        self.ref, self.start = ref, start

    def __getitem__(self, at):
        return self.ref[at[0], self.start + at[1]]


def split_table(table):
    return tuple(Column(table, 3 * i) for i in range(4))


def plain(*shape):
    return jax.ShapeDtypeStruct(shape, jnp.float32)


def far_off(*shape):
    return pltpu.HBM(shape, jnp.float32)


def f32(*shape):
    return pltpu.VMEM(shape, jnp.float32)


class Near:
    def __init__(self, x):
        self.x = pltpu.with_memory_space_constraint(x, pltpu.VMEM)


def near(x):
    return x.x if isinstance(x, Near) else Near(x).x


def call(body, ins, outs, name, scratch=()):
    run = pl.pallas_call(
        body,
        in_specs=ins,
        out_specs=[VM] * len(outs),
        out_shape=outs,
        scratch_shapes=list(scratch),
        name=name,
        compiler_params=pltpu.CompilerParams(vmem_limit_bytes=8 * 1024 * 1024),
    )

    def placed(*args):
        return run(*(near(x) if s is VM else x for s, x in zip(ins, args)))

    return placed


def lanes(rows=LOADS):
    return lax.broadcasted_iota(jnp.int32, (rows, FACE), 1)


def region(colour):
    return slice((2 + colour) * FACE, (3 + colour) * FACE)


def slot(half, peer):
    return pl.ds(pl.multiple_of((half * PEERS + peer) * LOADS, LOADS), LOADS)


def own_peer():
    return lax.axis_index("x") * NC + lax.axis_index("c")


def pack(pieces, partner, offset, length, buf, far):
    half = lax.axis_index("v")
    even = half == 0
    far[...] = jnp.where(even, pieces[0], pieces[1])
    buf[...] = jnp.zeros(buf.shape, jnp.float32)
    buf[slot(1 - half, own_peer()), :] = jnp.where(even, pieces[1], pieces[0])
    for k in range(COLOURS):
        turn = (FACE - offset[0, k]) % FACE
        rolled = pltpu.roll(pieces[2 + k], turn, 1)
        out = jnp.where(lanes() < length[0, k], rolled, 0.0)
        buf[slot(half, partner[0, k]), :] = out


def inside(offset, length, k):
    at = lanes()
    return (at >= offset[0, k]) & (at < offset[0, k] + length[0, k])


def weights(offset, length):
    sub = lax.axis_index("y") * NZ + lax.axis_index("u") * NV + lax.axis_index("v")
    parts = [
        jnp.where(sub > 0, 0.5, 1.0),
        jnp.where(sub < NY * NZ - 1, 0.5, 1.0),
    ]
    for k in range(COLOURS):
        parts.append(jnp.where(inside(offset, length, k), 0.5, 1.0))
    return parts


def assembled(values, recv, far, partner, offset, length):
    half = lax.axis_index("v")
    even = half == 0
    near_face = recv[slot(1 - half, own_peer()), :]
    far_face = far[...]
    below = jnp.where(even, far_face, near_face)
    above = jnp.where(even, near_face, far_face)
    parts = [values[:, :FACE] + below, values[:, FACE : 2 * FACE] + above]
    for k in range(COLOURS):
        turned = pltpu.roll(recv[slot(half, partner[0, k]), :], offset[0, k], 1)
        parts.append(
            values[:, region(k)] + jnp.where(inside(offset, length, k), turned, 0.0)
        )
    return parts


def pack_body(values, basis, partner, offset, length, buf, far, values_out, basis_out):
    values_out[...] = values[...]
    basis_out[...] = basis[...]
    pieces = [values[:, i * FACE : (i + 1) * FACE] for i in range(5)]
    pack(pieces, partner, offset, length, buf, far)


def constraint_row(a, basis):
    tiled = jnp.concatenate([a] * CONS, axis=0)
    prod = lax.dot_general(
        basis[...],
        tiled,
        (((1,), (1,)), ((), ())),
        precision=highest,
        preferred_element_type=jnp.float32,
    )
    row = lax.broadcasted_iota(jnp.int32, (CONS, FACE), 0)
    own = lanes(CONS) // LOADS == row
    return jnp.sum(jnp.where(own, prod, 0.0), axis=0, keepdims=True)


def scaled_body(first, *refs):
    values, recv, far, table, basis, a_out, msg = refs
    partner, offset, length, index = split_table(table)
    parts = assembled(values, recv, far, partner, offset, length)
    parts = [w * p for w, p in zip(weights(offset, length), parts)]
    a = jnp.concatenate(parts, axis=1)
    a_out[...] = a
    row = jnp.broadcast_to(constraint_row(a, basis), (8, FACE))
    if first:
        place = lax.axis_index("u") * NV + lax.axis_index("v")
        at = lanes(8)
        marks = jnp.zeros((8, FACE), jnp.float32)
        for j in range(CONS):
            marks = jnp.where(at == j * 16 + place, index[0, j].astype(jnp.float32), marks)
        odd = lax.broadcasted_iota(jnp.int32, (8, FACE), 0) % 2 == 1
        row = jnp.where(odd, marks, row)
    for t in range(0, msg.shape[0], 8):
        top = min(t + 8, msg.shape[0])
        msg[t:top, :] = row[: top - t]


def spread_body(first, got, out):
    if first:
        cons = got[pl.ds(0, NZ, 2), :]
        marks = jnp.sum(got[pl.ds(1, NZ, 2), :], axis=0, keepdims=True)
        block = jnp.concatenate([cons, marks, jnp.zeros((3, FACE), jnp.float32)], axis=0)
        for t in range(GROUP):
            out[16 * t : 16 * t + 16, :] = block
    else:
        twice = jnp.concatenate([got[pl.ds(0, NZ, 2), :]] * 2, axis=0)
        for t in range(GROUP // 2):
            out[24 * t : 24 * t + 24, :] = twice


def lane_take(x, idx):
    return jnp.take_along_axis(x, idx, axis=1, mode="promise_in_bounds")


def select_into(own, other, rows, sel, want, cons):
    lane = lanes(8)
    row = lax.broadcasted_iota(jnp.int32, (8, FACE), 0)
    for half, src in enumerate((own, other)):
        for g in range(GROUP):
            to = half * HALF + g * NZ
            cons[to : to + NZ, :] = src[16 * g : 16 * g + NZ, :]
        for block in range(3):
            at = lane + block * FACE
            group, where = at // NZ, row * 16 + at % NZ
            acc = jnp.zeros((8, FACE), jnp.float32)
            for g in range(block * FACE // NZ, ((block + 1) * FACE - 1) // NZ + 1):
                line = jnp.broadcast_to(src[16 * g + NZ : 16 * g + NZ + 1, :], (8, FACE))
                acc = jnp.where(group == g, lane_take(line, where), acc)
            to = (half * 3 + block) * 8
            want[to : to + 8, :] = acc.astype(jnp.int32)

    def step(t, carry):
        for k in range(4):
            at = t * 4 + k
            line = jnp.broadcast_to(want[pl.ds(at, 1), :], (8, FACE))
            high = line // FACE
            low = line % FACE
            acc = jnp.zeros((8, FACE), jnp.float32)
            for ch in range(CHUNKS):
                part = lane_take(rows[:, ch * FACE : (ch + 1) * FACE], low)
                acc = jnp.where(high == ch, part, acc)
            sel[pl.ds(pl.multiple_of(at * 8, 8), 8), :] = acc
        return carry

    lax.fori_loop(0, CHUNKS // 4, step, 0)


def coarse_part(cons, sel):
    wide = jnp.concatenate([sel[64 * b : 64 * b + 64, :] for b in range(6)], axis=1)
    full = jnp.dot(wide, cons, precision=highest, preferred_element_type=jnp.float32)
    group = lanes(8) // LOADS
    acc = jnp.zeros((8, FACE), jnp.float32)
    for j in range(CONS):
        acc = jnp.where(group == j, full[8 * j : 8 * j + 8, :], acc)
    fold = lax.broadcasted_iota(jnp.int32, (LOADS, FACE), 0) == lanes() % LOADS
    return lax.dot_general(
        jnp.where(fold, 1.0, 0.0),
        acc,
        (((1,), (1,)), ((), ())),
        precision=highest,
        preferred_element_type=jnp.float32,
    )


def local_body(first, *refs):
    if first:
        own, other, rows, local, basis, table, w_out, buf, far, sel, want, cons = refs
        select_into(own, other, rows, sel, want, cons)
        gathered = cons[...]
    else:
        own, other, sel, local, basis, table, w_out, buf, far = refs
        gathered = jnp.concatenate([own[...], other[...]], axis=0)
    partner, offset, length, _ = split_table(table)
    coarse = coarse_part(gathered, sel)
    full = local[...] + jnp.dot(
        coarse, basis[...], precision=highest, preferred_element_type=jnp.float32
    )
    scale = weights(offset, length)
    parts = [scale[i] * full[:, i * FACE : (i + 1) * FACE] for i in range(5)]
    w_out[...] = jnp.concatenate(parts, axis=1)
    pack(parts, partner, offset, length, buf, far)


def halves(x):
    top = x.astype(jnp.bfloat16)
    return top, (x - top.astype(jnp.float32)).astype(jnp.bfloat16)


def minus_product(base, step, schur):
    top, rest = halves(step)
    s_top, s_rest = halves(schur[...])
    both = jnp.dot(
        jnp.concatenate([top, rest], axis=0), s_top, preferred_element_type=jnp.float32
    )
    small = jnp.dot(top, s_rest, preferred_element_type=jnp.float32)
    return base[...] - (both[:LOADS] + (both[LOADS:] + small))


def step_body(first, *refs):
    *refs, matrix, sem = refs
    values, recv, far, table, residual, schur, *rest = refs
    fetch = pltpu.make_async_copy(schur, matrix, sem)
    fetch.start()
    partner, offset, length, _ = split_table(table)
    new = jnp.concatenate(assembled(values, recv, far, partner, offset, length), axis=1)
    if first:
        step, left, buf, far_out = rest
        new = new / THETA
        step[...] = new
        fetch.wait()
        out = minus_product(residual, new, matrix)
        left[...] = out
        pack(
            [out[:, i * FACE : (i + 1) * FACE] for i in range(5)],
            partner, offset, length, buf, far_out,
        )
    else:
        prev, total, left = rest
        new = (RHO1 * RHO0) * prev[...] + (2.0 * RHO1 / DELTA) * new
        total[...] = prev[...] + new
        fetch.wait()
        left[...] = minus_product(residual, new, matrix)


def product(left, right):
    return jnp.dot(left, right, precision=highest, preferred_element_type=jnp.float32)


def per_device(
    loads, schur, local_inverse, coarse_basis, coarse_rows, partner, offset, length, index
):
    firsts = [
        pltpu.with_memory_space_constraint(x, pltpu.HBM)
        for x in (loads, coarse_basis, partner, offset, length)
    ]
    schur = pltpu.with_memory_space_constraint(schur, pltpu.HBM)
    table = jnp.concatenate([partner, offset, length, index], axis=1)
    odd = range(1, NY * NZ - 1, 2)
    pairs = [(i, i + 1) for i in odd] + [(i + 1, i) for i in odd]
    packed_outs = [far_off(NV * PEERS * LOADS, FACE), far_off(LOADS, FACE)]

    def exchange(buf, far):
        recv = lax.all_to_all(
            buf.reshape(NV * PEERS, LOADS, FACE), PAIR, split_axis=0, concat_axis=0, tiled=True
        )
        return recv.reshape(NV * PEERS * LOADS, FACE), lax.ppermute(far, SUB, pairs)

    def precondition(packed, residual, first, sel, basis):
        recv, far = exchange(*packed)
        per = 2
        ins = [VM, VM, VM, SM, VM]
        a, msg = call(
            functools.partial(scaled_body, first),
            ins,
            [f32(LOADS, ORDER), f32(NZ * per, FACE)],
            "scaled",
        )(residual, recv, far, table, basis)
        got = lax.all_to_all(
            msg.reshape(NZ, per, FACE), LINE, split_axis=0, concat_axis=0, tiled=True
        )
        pitch = 16 if first else NZ
        (wide,) = call(
            functools.partial(spread_body, first), [VM], [f32(GROUP * pitch, FACE)], "spread"
        )(got.reshape(NZ * per, FACE))
        own = lax.all_to_all(
            wide.reshape(GROUP, pitch // 4, 4, FACE), ("y", "x"), split_axis=0, concat_axis=0, tiled=True
        ).reshape(GROUP * pitch, FACE)
        other = lax.ppermute(own, "c", [(0, 1), (1, 0)])
        local = product(a, local_inverse)
        outs = [f32(LOADS, ORDER)] + packed_outs
        scratch = []
        third = coarse_rows if first else sel
        if first:
            outs = outs + [far_off(CHUNKS * 8, FACE)]
            scratch = [pltpu.VMEM((CHUNKS, FACE), jnp.int32), f32(2 * HALF, FACE)]
        res = call(
            functools.partial(local_body, first),
            [VM, VM, VM, VM, VM, SM],
            outs,
            "local",
            scratch,
        )(own, other, third, local, basis, table)
        if first:
            sel = res[3]
        return (res[0], *exchange(*res[1:3])), sel

    base = [VM, VM, VM, SM, VM, HB]
    held = [f32(ORDER, ORDER), pltpu.SemaphoreType.DMA(())]
    buf, far, loads, basis = call(
        pack_body,
        [LATE, LATE, SM, SM, SM],
        packed_outs + [f32(LOADS, ORDER), f32(CONS, ORDER)],
        "pack",
    )(*firsts)
    packed = (buf, far)
    done, sel = precondition(packed, loads, True, None, basis)
    step, residual, *packed = call(
        functools.partial(step_body, True),
        base,
        [f32(LOADS, ORDER), f32(LOADS, ORDER)] + packed_outs,
        "step",
        held,
    )(*done, table, loads, schur)
    done, sel = precondition(packed, residual, False, sel, basis)
    ends = [plain(LOADS, ORDER)] * 2
    return tuple(
        call(functools.partial(step_body, False), base + [VM], ends, "step", held)(
            *done, table, residual, schur, step
        )
    )


def solution(mesh):
    finer = Mesh(mesh.devices.reshape(NY, NZ // NV, NV, NX, NC), ALL)
    spec = P(ALL, None)
    return jax.shard_map(
        per_device, mesh=finer, in_specs=(spec,) * 9, out_specs=(spec, spec), check_vma=False
    )
```

```python
import functools

import jax
import jax.numpy as jnp
from jax import lax
from jax.experimental import pallas as pl
from jax.experimental.pallas import tpu as pltpu
from jax.sharding import Mesh
from jax.sharding import PartitionSpec as P

FACE = 128
COLOURS = 3
ORDER = 640
LOADS = 16
CONS = 8
NY, NZ, NX, NC = 8, 12, 4, 2
NV = 2
PEERS = NX * NC
GROUP = NY * NX
HALF = NZ * GROUP
CHUNKS = 48
WIDE = NZ + 1
LINE = ("u", "v")
SUB = ("y", "u", "v")
PAIR = ("v", "x", "c")
ALL = ("y", "u", "v", "x", "c")

highest = lax.Precision.HIGHEST
LOW, HIGH = 0.5, 4.0
THETA = (HIGH + LOW) / 2.0
DELTA = (HIGH - LOW) / 2.0
SIGMA = THETA / DELTA
RHO0 = 1.0 / SIGMA
RHO1 = 1.0 / (2.0 * SIGMA - RHO0)

VM = pl.BlockSpec(memory_space=pltpu.VMEM)
SM = pl.BlockSpec(memory_space=pltpu.SMEM)
LATE = pl.BlockSpec(memory_space=pltpu.VMEM)
HB = pl.BlockSpec(memory_space=pl.ANY)


class Column:
    def __init__(self, ref, start):
        self.ref, self.start = ref, start

    def __getitem__(self, at):
        return self.ref[at[0], self.start + at[1]]


def split_table(table):
    return tuple(Column(table, 3 * i) for i in range(4))


def plain(*shape):
    return jax.ShapeDtypeStruct(shape, jnp.float32)


def far_off(*shape):
    return pltpu.HBM(shape, jnp.float32)


def f32(*shape):
    return pltpu.VMEM(shape, jnp.float32)


class Near:
    def __init__(self, x):
        self.x = pltpu.with_memory_space_constraint(x, pltpu.VMEM)


def near(x):
    return x.x if isinstance(x, Near) else Near(x).x


def call(body, ins, outs, name, scratch=()):
    run = pl.pallas_call(
        body,
        in_specs=ins,
        out_specs=[VM] * len(outs),
        out_shape=outs,
        scratch_shapes=list(scratch),
        name=name,
        compiler_params=pltpu.CompilerParams(vmem_limit_bytes=8 * 1024 * 1024),
    )

    def placed(*args):
        return run(*(near(x) if s is VM else x for s, x in zip(ins, args)))

    return placed


def halves(x):
    top = x.astype(jnp.bfloat16)
    return top, (x - top.astype(jnp.float32)).astype(jnp.bfloat16)


def split_product(left, right, across=0):
    dims = (((1,), (across,)), ((), ()))
    top, rest = halves(left)
    r_top, r_rest = halves(right)
    both = lax.dot_general(
        jnp.concatenate([top, rest], axis=0), r_top, dims, preferred_element_type=jnp.float32
    )
    small = lax.dot_general(top, r_rest, dims, preferred_element_type=jnp.float32)
    size = left.shape[0]
    return both[:size] + (both[size:] + small)


def lanes(rows=LOADS):
    return lax.broadcasted_iota(jnp.int32, (rows, FACE), 1)


def region(colour):
    return slice((2 + colour) * FACE, (3 + colour) * FACE)


def slot(half, peer):
    return pl.ds(pl.multiple_of((half * PEERS + peer) * LOADS, LOADS), LOADS)


def own_peer():
    return lax.axis_index("x") * NC + lax.axis_index("c")


def pack(pieces, partner, offset, length, buf, far):
    half = lax.axis_index("v")
    even = half == 0
    far[...] = jnp.where(even, pieces[0], pieces[1])
    buf[...] = jnp.zeros(buf.shape, jnp.float32)
    buf[slot(1 - half, own_peer()), :] = jnp.where(even, pieces[1], pieces[0])
    for k in range(COLOURS):
        turn = (FACE - offset[0, k]) % FACE
        rolled = pltpu.roll(pieces[2 + k], turn, 1)
        out = jnp.where(lanes() < length[0, k], rolled, 0.0)
        buf[slot(half, partner[0, k]), :] = out


def inside(offset, length, k):
    at = lanes()
    return (at >= offset[0, k]) & (at < offset[0, k] + length[0, k])


def weights(offset, length):
    sub = lax.axis_index("y") * NZ + lax.axis_index("u") * NV + lax.axis_index("v")
    parts = [
        jnp.where(sub > 0, 0.5, 1.0),
        jnp.where(sub < NY * NZ - 1, 0.5, 1.0),
    ]
    for k in range(COLOURS):
        parts.append(jnp.where(inside(offset, length, k), 0.5, 1.0))
    return parts


def assembled(values, recv, far, partner, offset, length):
    half = lax.axis_index("v")
    even = half == 0
    near_face = recv[slot(1 - half, own_peer()), :]
    far_face = far[...]
    below = jnp.where(even, far_face, near_face)
    above = jnp.where(even, near_face, far_face)
    parts = [values[:, :FACE] + below, values[:, FACE : 2 * FACE] + above]
    for k in range(COLOURS):
        turned = pltpu.roll(recv[slot(half, partner[0, k]), :], offset[0, k], 1)
        parts.append(
            values[:, region(k)] + jnp.where(inside(offset, length, k), turned, 0.0)
        )
    return parts


def pack_body(values, basis, partner, offset, length, buf, far, values_out, basis_out):
    values_out[...] = values[...]
    basis_out[...] = basis[...]
    pieces = [values[:, i * FACE : (i + 1) * FACE] for i in range(5)]
    pack(pieces, partner, offset, length, buf, far)


def constraint_row(a, basis):
    tiled = jnp.concatenate([a] * CONS, axis=0)
    double = jnp.concatenate([basis[...]] * 2, axis=0)
    prod = split_product(double, tiled, 1)[:CONS]
    row = lax.broadcasted_iota(jnp.int32, (CONS, FACE), 0)
    own = lanes(CONS) // LOADS == row
    return jnp.sum(jnp.where(own, prod, 0.0), axis=0, keepdims=True)


def scaled_body(first, *refs):
    values, recv, far, table, basis, a_out, msg = refs
    partner, offset, length, index = split_table(table)
    parts = assembled(values, recv, far, partner, offset, length)
    parts = [w * p for w, p in zip(weights(offset, length), parts)]
    a = jnp.concatenate(parts, axis=1)
    a_out[...] = a
    row = jnp.broadcast_to(constraint_row(a, basis), (8, FACE))
    if first:
        place = lax.axis_index("u") * NV + lax.axis_index("v")
        at = lanes(8)
        marks = jnp.zeros((8, FACE), jnp.float32)
        for j in range(CONS):
            marks = jnp.where(at == j * 16 + place, index[0, j].astype(jnp.float32), marks)
        odd = lax.broadcasted_iota(jnp.int32, (8, FACE), 0) % 2 == 1
        row = jnp.where(odd, marks, row)
    for t in range(0, msg.shape[0], 8):
        top = min(t + 8, msg.shape[0])
        msg[t:top, :] = row[: top - t]


def spread_body(first, got, out):
    if first:
        cons = got[pl.ds(0, NZ, 2), :]
        marks = jnp.sum(got[pl.ds(1, NZ, 2), :], axis=0, keepdims=True)
        block = jnp.concatenate([cons, marks], axis=0)
        for t in range(GROUP):
            out[WIDE * t : WIDE * (t + 1), :] = block
    else:
        twice = jnp.concatenate([got[pl.ds(0, NZ, 2), :]] * 2, axis=0)
        for t in range(GROUP // 2):
            out[24 * t : 24 * t + 24, :] = twice


def lane_take(x, idx):
    return jnp.take_along_axis(x, idx, axis=1, mode="promise_in_bounds")


def select_into(src, rows, sel, cons, want):
    lane = lanes(8)
    row = lax.broadcasted_iota(jnp.int32, (8, FACE), 0)
    for g in range(GROUP):
        cons[g * NZ : (g + 1) * NZ, :] = src[WIDE * g : WIDE * g + NZ, :]
    for block in range(3):
        at = lane + block * FACE
        group, where = at // NZ, row * 16 + at % NZ
        acc = jnp.zeros((8, FACE), jnp.float32)
        for g in range(block * FACE // NZ, ((block + 1) * FACE - 1) // NZ + 1):
            line = jnp.broadcast_to(src[WIDE * g + NZ : WIDE * (g + 1), :], (8, FACE))
            acc = jnp.where(group == g, lane_take(line, where), acc)
        want[block * 8 : block * 8 + 8, :] = acc.astype(jnp.int32)

    def step(t, carry):
        for k in range(4):
            at = t * 4 + k
            line = jnp.broadcast_to(want[pl.ds(at, 1), :], (8, FACE))
            high = line // FACE
            low = line % FACE
            acc = jnp.zeros((8, FACE), jnp.float32)
            for ch in range(CHUNKS):
                part = lane_take(rows[:, ch * FACE : (ch + 1) * FACE], low)
                acc = jnp.where(high == ch, part, acc)
            sel[pl.ds(pl.multiple_of(at * 8, 8), 8), :] = acc
        return carry

    lax.fori_loop(0, 6, step, 0)


def coarse_part(cons, sels):
    blocks = [sel[64 * b : 64 * b + 64, :] for sel in sels for b in range(3)]
    full = split_product(jnp.concatenate(blocks, axis=1), cons)
    group = lanes(8) // LOADS
    acc = jnp.zeros((8, FACE), jnp.float32)
    for j in range(CONS):
        acc = jnp.where(group == j, full[8 * j : 8 * j + 8, :], acc)
    fold = lax.broadcasted_iota(jnp.int32, (LOADS, FACE), 0) == lanes() % LOADS
    return lax.dot_general(
        jnp.where(fold, 1.0, 0.0),
        acc,
        (((1,), (1,)), ((), ())),
        precision=highest,
        preferred_element_type=jnp.float32,
    )


def local_body(first, *refs):
    if first:
        (cons_own, sel_own, other, rows, local, basis, table,
         w_out, buf, far, sel, cons, want) = refs
        select_into(other, rows, sel, cons, want)
        gathered = jnp.concatenate([cons_own[...], cons[...]], axis=0)
    else:
        own, sel_own, other, sel, local, basis, table, w_out, buf, far = refs
        gathered = jnp.concatenate([own[...], other[...]], axis=0)
    partner, offset, length, _ = split_table(table)
    coarse = coarse_part(gathered, (sel_own, sel))
    full = local[...] + split_product(coarse, basis[...])
    scale = weights(offset, length)
    parts = [scale[i] * full[:, i * FACE : (i + 1) * FACE] for i in range(5)]
    w_out[...] = jnp.concatenate(parts, axis=1)
    pack(parts, partner, offset, length, buf, far)


def inverse_body(a, inverse, out, matrix, sem):
    fetch = pltpu.make_async_copy(inverse, matrix, sem)
    fetch.start()
    fetch.wait()
    out[...] = split_product(a[...], matrix[...])


def step_body(first, *refs):
    values, recv, far, table, residual, schur, *rest = refs
    partner, offset, length, _ = split_table(table)
    new = jnp.concatenate(assembled(values, recv, far, partner, offset, length), axis=1)
    if first:
        step, left, buf, far_out = rest
        new = new / THETA
        step[...] = new
        out = residual[...] - split_product(new, schur[...])
        left[...] = out
        pack(
            [out[:, i * FACE : (i + 1) * FACE] for i in range(5)],
            partner, offset, length, buf, far_out,
        )
    else:
        prev, total, left = rest
        new = (RHO1 * RHO0) * prev[...] + (2.0 * RHO1 / DELTA) * new
        total[...] = prev[...] + new
        left[...] = residual[...] - split_product(new, schur[...])


def per_device(
    loads, schur, local_inverse, coarse_basis, coarse_rows, partner, offset, length, index
):
    firsts = [
        pltpu.with_memory_space_constraint(x, pltpu.HBM)
        for x in (loads, coarse_basis, partner, offset, length)
    ]
    schur = Near(schur)
    coarse_rows = Near(coarse_rows)
    local_inverse = pltpu.with_memory_space_constraint(local_inverse, pltpu.HBM)
    table = jnp.concatenate([partner, offset, length, index], axis=1)
    odd = range(1, NY * NZ - 1, 2)
    pairs = [(i, i + 1) for i in odd] + [(i + 1, i) for i in odd]
    packed_outs = [far_off(NV * PEERS * LOADS, FACE), far_off(LOADS, FACE)]

    def exchange(buf, far):
        recv = lax.all_to_all(
            buf.reshape(NV * PEERS, LOADS, FACE), PAIR, split_axis=0, concat_axis=0, tiled=True
        )
        return recv.reshape(NV * PEERS * LOADS, FACE), lax.ppermute(far, SUB, pairs)

    def precondition(packed, residual, first, sel, basis):
        recv, far = exchange(*packed)
        per = 2
        ins = [VM, VM, VM, SM, VM]
        a, msg = call(
            functools.partial(scaled_body, first),
            ins,
            [f32(LOADS, ORDER), f32(NZ * per, FACE)],
            "scaled",
        )(residual, recv, far, table, basis)
        got = lax.all_to_all(
            msg.reshape(NZ, per, FACE), LINE, split_axis=0, concat_axis=0, tiled=True
        )
        (local,) = call(
            inverse_body,
            [VM, HB],
            [f32(LOADS, ORDER)],
            "inverse",
            [f32(ORDER, ORDER), pltpu.SemaphoreType.DMA(())],
        )(a, local_inverse)
        got, local = lax.optimization_barrier((got, local))
        pitch, tile = (WIDE, 1) if first else (NZ, 4)
        (wide,) = call(
            functools.partial(spread_body, first), [VM], [f32(GROUP * pitch, FACE)], "spread"
        )(got.reshape(NZ * per, FACE))
        own = lax.all_to_all(
            wide.reshape(GROUP, pitch // tile, tile, FACE), ("y", "x"), split_axis=0, concat_axis=0, tiled=True
        ).reshape(GROUP * pitch, FACE)
        other = lax.ppermute(own, "c", [(0, 1), (1, 0)])
        outs = [f32(LOADS, ORDER)] + packed_outs
        scratch = []
        lines = pltpu.VMEM((CHUNKS // 2, FACE), jnp.int32)
        half_rows = CHUNKS // 2 * 8
        if first:
            chosen, own = call(
                select_into, [VM, VM], [f32(half_rows, FACE), f32(HALF, FACE)], "select", [lines]
            )(own, coarse_rows)
            outs = outs + [f32(half_rows, FACE)]
            scratch = [f32(HALF, FACE), lines]
            third = coarse_rows
        else:
            chosen, third = sel
        res = call(
            functools.partial(local_body, first),
            [VM, VM, VM, VM, VM, VM, SM],
            outs,
            "local",
            scratch,
        )(own, chosen, other, third, local, basis, table)
        if first:
            sel = (chosen, res[3])
        return (res[0], *exchange(*res[1:3])), sel

    base = [VM, VM, VM, SM, VM, VM]
    buf, far, loads, basis = call(
        pack_body,
        [LATE, LATE, SM, SM, SM],
        packed_outs + [f32(LOADS, ORDER), f32(CONS, ORDER)],
        "pack",
    )(*firsts)
    packed = (buf, far)
    done, sel = precondition(packed, loads, True, None, basis)
    step, residual, *packed = call(
        functools.partial(step_body, True),
        base,
        [f32(LOADS, ORDER), f32(LOADS, ORDER)] + packed_outs,
        "step",
    )(*done, table, loads, schur)
    done, sel = precondition(packed, residual, False, sel, basis)
    ends = [plain(LOADS, ORDER)] * 2
    return tuple(
        call(functools.partial(step_body, False), base + [VM], ends, "step")(
            *done, table, residual, schur, step
        )
    )


def solution(mesh):
    finer = Mesh(mesh.devices.reshape(NY, NZ // NV, NV, NX, NC), ALL)
    spec = P(ALL, None)
    return jax.shard_map(
        per_device, mesh=finer, in_specs=(spec,) * 9, out_specs=(spec, spec), check_vma=False
    )
```

```python
import functools

import jax
import jax.numpy as jnp
from jax import lax
from jax.experimental import pallas as pl
from jax.experimental.pallas import tpu as pltpu
from jax.sharding import Mesh
from jax.sharding import PartitionSpec as P

FACE = 128
COLOURS = 3
ORDER = 640
LOADS = 16
CONS = 8
NY, NZ, NX, NC = 8, 12, 4, 2
NV = 2
PEERS = NX * NC
GROUP = NY * NX
HALF = NZ * GROUP
CHUNKS = 48
WIDE = NZ + 1
LINE = ("u", "v")
SUB = ("y", "u", "v")
PAIR = ("v", "x", "c")
ALL = ("y", "u", "v", "x", "c")

highest = lax.Precision.HIGHEST
LOW, HIGH = 0.5, 4.0
THETA = (HIGH + LOW) / 2.0
DELTA = (HIGH - LOW) / 2.0
SIGMA = THETA / DELTA
RHO0 = 1.0 / SIGMA
RHO1 = 1.0 / (2.0 * SIGMA - RHO0)

VM = pl.BlockSpec(memory_space=pltpu.VMEM)
SM = pl.BlockSpec(memory_space=pltpu.SMEM)
LATE = pl.BlockSpec(memory_space=pltpu.VMEM)
HB = pl.BlockSpec(memory_space=pl.ANY)


class Column:
    def __init__(self, ref, start):
        self.ref, self.start = ref, start

    def __getitem__(self, at):
        return self.ref[at[0], self.start + at[1]]


def split_table(table):
    return tuple(Column(table, 3 * i) for i in range(4))


def plain(*shape):
    return jax.ShapeDtypeStruct(shape, jnp.float32)


def far_off(*shape):
    return pltpu.HBM(shape, jnp.float32)


def f32(*shape):
    return pltpu.VMEM(shape, jnp.float32)


class Near:
    def __init__(self, x):
        self.x = pltpu.with_memory_space_constraint(x, pltpu.VMEM)


def near(x):
    return x.x if isinstance(x, Near) else Near(x).x


def call(body, ins, outs, name, scratch=()):
    run = pl.pallas_call(
        body,
        in_specs=ins,
        out_specs=[VM] * len(outs),
        out_shape=outs,
        scratch_shapes=list(scratch),
        name=name,
        compiler_params=pltpu.CompilerParams(vmem_limit_bytes=8 * 1024 * 1024),
    )

    def placed(*args):
        return run(*(near(x) if s is VM else x for s, x in zip(ins, args)))

    return placed


def halves(x):
    top = x.astype(jnp.bfloat16)
    return top, (x - top.astype(jnp.float32)).astype(jnp.bfloat16)


def split_product(left, right, across=0):
    dims = (((1,), (across,)), ((), ()))
    top, rest = halves(left)
    r_top, r_rest = halves(right)
    both = lax.dot_general(
        jnp.concatenate([top, rest], axis=0), r_top, dims, preferred_element_type=jnp.float32
    )
    small = lax.dot_general(top, r_rest, dims, preferred_element_type=jnp.float32)
    size = left.shape[0]
    return both[:size] + (both[size:] + small)


def lanes(rows=LOADS):
    return lax.broadcasted_iota(jnp.int32, (rows, FACE), 1)


def region(colour):
    return slice((2 + colour) * FACE, (3 + colour) * FACE)


def slot(half, peer):
    return pl.ds(pl.multiple_of((half * PEERS + peer) * LOADS, LOADS), LOADS)


def own_peer():
    return lax.axis_index("x") * NC + lax.axis_index("c")


def pack(pieces, partner, offset, length, buf, far):
    half = lax.axis_index("v")
    even = half == 0
    far[...] = jnp.where(even, pieces[0], pieces[1])
    buf[...] = jnp.zeros(buf.shape, jnp.float32)
    buf[slot(1 - half, own_peer()), :] = jnp.where(even, pieces[1], pieces[0])
    for k in range(COLOURS):
        turn = (FACE - offset[0, k]) % FACE
        rolled = pltpu.roll(pieces[2 + k], turn, 1)
        out = jnp.where(lanes() < length[0, k], rolled, 0.0)
        buf[slot(half, partner[0, k]), :] = out


def inside(offset, length, k):
    at = lanes()
    return (at >= offset[0, k]) & (at < offset[0, k] + length[0, k])


def weights(offset, length):
    sub = lax.axis_index("y") * NZ + lax.axis_index("u") * NV + lax.axis_index("v")
    parts = [
        jnp.where(sub > 0, 0.5, 1.0),
        jnp.where(sub < NY * NZ - 1, 0.5, 1.0),
    ]
    for k in range(COLOURS):
        parts.append(jnp.where(inside(offset, length, k), 0.5, 1.0))
    return parts


def assembled(values, recv, far, partner, offset, length):
    half = lax.axis_index("v")
    even = half == 0
    near_face = recv[slot(1 - half, own_peer()), :]
    far_face = far[...]
    below = jnp.where(even, far_face, near_face)
    above = jnp.where(even, near_face, far_face)
    parts = [values[:, :FACE] + below, values[:, FACE : 2 * FACE] + above]
    for k in range(COLOURS):
        turned = pltpu.roll(recv[slot(half, partner[0, k]), :], offset[0, k], 1)
        parts.append(
            values[:, region(k)] + jnp.where(inside(offset, length, k), turned, 0.0)
        )
    return parts


def pack_body(values, basis, partner, offset, length, buf, far, values_out, basis_out):
    values_out[...] = values[...]
    basis_out[...] = basis[...]
    pieces = [values[:, i * FACE : (i + 1) * FACE] for i in range(5)]
    pack(pieces, partner, offset, length, buf, far)


def constraint_row(a, basis):
    tiled = jnp.concatenate([a] * CONS, axis=0)
    prod = lax.dot_general(
        basis[...],
        tiled,
        (((1,), (1,)), ((), ())),
        precision=highest,
        preferred_element_type=jnp.float32,
    )
    row = lax.broadcasted_iota(jnp.int32, (CONS, FACE), 0)
    own = lanes(CONS) // LOADS == row
    return jnp.sum(jnp.where(own, prod, 0.0), axis=0, keepdims=True)


def scaled_body(first, *refs):
    values, recv, far, table, basis, a_out, msg = refs
    partner, offset, length, index = split_table(table)
    parts = assembled(values, recv, far, partner, offset, length)
    parts = [w * p for w, p in zip(weights(offset, length), parts)]
    a = jnp.concatenate(parts, axis=1)
    a_out[...] = a
    row = jnp.broadcast_to(constraint_row(a, basis), (8, FACE))
    if first:
        place = lax.axis_index("u") * NV + lax.axis_index("v")
        at = lanes(8)
        marks = jnp.zeros((8, FACE), jnp.float32)
        for j in range(CONS):
            marks = jnp.where(at == j * 16 + place, index[0, j].astype(jnp.float32), marks)
        odd = lax.broadcasted_iota(jnp.int32, (8, FACE), 0) % 2 == 1
        row = jnp.where(odd, marks, row)
    for t in range(0, msg.shape[0], 8):
        top = min(t + 8, msg.shape[0])
        msg[t:top, :] = row[: top - t]


def spread_body(first, got, out):
    if first:
        cons = got[pl.ds(0, NZ, 2), :]
        marks = jnp.sum(got[pl.ds(1, NZ, 2), :], axis=0, keepdims=True)
        block = jnp.concatenate([cons, marks], axis=0)
        for t in range(GROUP):
            out[WIDE * t : WIDE * (t + 1), :] = block
    else:
        twice = jnp.concatenate([got[pl.ds(0, NZ, 2), :]] * 2, axis=0)
        for t in range(GROUP // 2):
            out[24 * t : 24 * t + 24, :] = twice


def lane_take(x, idx):
    return jnp.take_along_axis(x, idx, axis=1, mode="promise_in_bounds")


def select_into(src, rows, sel, cons, want):
    lane = lanes(8)
    row = lax.broadcasted_iota(jnp.int32, (8, FACE), 0)
    for g in range(GROUP):
        cons[g * NZ : (g + 1) * NZ, :] = src[WIDE * g : WIDE * g + NZ, :]
    for block in range(3):
        at = lane + block * FACE
        group, where = at // NZ, row * 16 + at % NZ
        acc = jnp.zeros((8, FACE), jnp.float32)
        for g in range(block * FACE // NZ, ((block + 1) * FACE - 1) // NZ + 1):
            line = jnp.broadcast_to(src[WIDE * g + NZ : WIDE * (g + 1), :], (8, FACE))
            acc = jnp.where(group == g, lane_take(line, where), acc)
        want[block * 8 : block * 8 + 8, :] = acc.astype(jnp.int32)

    def step(t, carry):
        for k in range(4):
            at = t * 4 + k
            line = jnp.broadcast_to(want[pl.ds(at, 1), :], (8, FACE))
            high = line // FACE
            low = line % FACE
            acc = jnp.zeros((8, FACE), jnp.float32)
            for ch in range(CHUNKS):
                part = lane_take(rows[:, ch * FACE : (ch + 1) * FACE], low)
                acc = jnp.where(high == ch, part, acc)
            sel[pl.ds(pl.multiple_of(at * 8, 8), 8), :] = acc
        return carry

    lax.fori_loop(0, 6, step, 0)


def coarse_part(cons, sels):
    blocks = [sel[64 * b : 64 * b + 64, :] for sel in sels for b in range(3)]
    full = split_product(jnp.concatenate(blocks, axis=1), cons)
    group = lanes(8) // LOADS
    acc = jnp.zeros((8, FACE), jnp.float32)
    for j in range(CONS):
        acc = jnp.where(group == j, full[8 * j : 8 * j + 8, :], acc)
    fold = lax.broadcasted_iota(jnp.int32, (LOADS, FACE), 0) == lanes() % LOADS
    return lax.dot_general(
        jnp.where(fold, 1.0, 0.0),
        acc,
        (((1,), (1,)), ((), ())),
        precision=highest,
        preferred_element_type=jnp.float32,
    )


def local_body(first, *refs):
    if first:
        (cons_own, sel_own, other, rows, local, basis, table,
         w_out, buf, far, sel, cons, want) = refs
        select_into(other, rows, sel, cons, want)
        gathered = jnp.concatenate([cons_own[...], cons[...]], axis=0)
    else:
        own, sel_own, other, sel, local, basis, table, w_out, buf, far = refs
        gathered = jnp.concatenate([own[...], other[...]], axis=0)
    partner, offset, length, _ = split_table(table)
    coarse = coarse_part(gathered, (sel_own, sel))
    full = local[...] + split_product(coarse, basis[...])
    scale = weights(offset, length)
    parts = [scale[i] * full[:, i * FACE : (i + 1) * FACE] for i in range(5)]
    w_out[...] = jnp.concatenate(parts, axis=1)
    pack(parts, partner, offset, length, buf, far)


def inverse_body(a, inverse, out, matrix, sem):
    fetch = pltpu.make_async_copy(inverse, matrix, sem)
    fetch.start()
    fetch.wait()
    out[...] = split_product(a[...], matrix[...])


def step_body(first, *refs):
    values, recv, far, table, residual, schur, *rest = refs
    partner, offset, length, _ = split_table(table)
    new = jnp.concatenate(assembled(values, recv, far, partner, offset, length), axis=1)
    if first:
        step, left, buf, far_out = rest
        new = new / THETA
        step[...] = new
        out = residual[...] - split_product(new, schur[...])
        left[...] = out
        pack(
            [out[:, i * FACE : (i + 1) * FACE] for i in range(5)],
            partner, offset, length, buf, far_out,
        )
    else:
        prev, total, left = rest
        new = (RHO1 * RHO0) * prev[...] + (2.0 * RHO1 / DELTA) * new
        total[...] = prev[...] + new
        left[...] = residual[...] - split_product(new, schur[...])


def per_device(
    loads, schur, local_inverse, coarse_basis, coarse_rows, partner, offset, length, index
):
    firsts = [
        pltpu.with_memory_space_constraint(x, pltpu.HBM)
        for x in (loads, coarse_basis, partner, offset, length)
    ]
    schur = Near(schur)
    coarse_rows = Near(coarse_rows)
    local_inverse = pltpu.with_memory_space_constraint(local_inverse, pltpu.HBM)
    table = jnp.concatenate([partner, offset, length, index], axis=1)
    odd = range(1, NY * NZ - 1, 2)
    pairs = [(i, i + 1) for i in odd] + [(i + 1, i) for i in odd]
    packed_outs = [f32(NV * PEERS * LOADS, FACE), f32(LOADS, FACE)]

    def exchange(buf, far):
        recv = lax.all_to_all(
            buf.reshape(NV * PEERS, LOADS, FACE), PAIR, split_axis=0, concat_axis=0, tiled=True
        )
        return recv.reshape(NV * PEERS * LOADS, FACE), lax.ppermute(far, SUB, pairs)

    def precondition(packed, residual, first, sel, basis):
        recv, far = exchange(*packed)
        per = 2
        ins = [VM, VM, VM, SM, VM]
        a, msg = call(
            functools.partial(scaled_body, first),
            ins,
            [f32(LOADS, ORDER), f32(NZ * per, FACE)],
            "scaled",
        )(residual, recv, far, table, basis)
        got = lax.all_to_all(
            msg.reshape(NZ, per, FACE), LINE, split_axis=0, concat_axis=0, tiled=True
        )
        (local,) = call(
            inverse_body,
            [VM, HB],
            [f32(LOADS, ORDER)],
            "inverse",
            [f32(ORDER, ORDER), pltpu.SemaphoreType.DMA(())],
        )(a, local_inverse)
        got, local = lax.optimization_barrier((got, local))
        pitch, tile = (WIDE, 1) if first else (NZ, 4)
        (wide,) = call(
            functools.partial(spread_body, first), [VM], [f32(GROUP * pitch, FACE)], "spread"
        )(got.reshape(NZ * per, FACE))
        own = lax.all_to_all(
            wide.reshape(GROUP, pitch // tile, tile, FACE), ("y", "x"), split_axis=0, concat_axis=0, tiled=True
        ).reshape(GROUP * pitch, FACE)
        other = lax.ppermute(own, "c", [(0, 1), (1, 0)])
        outs = [f32(LOADS, ORDER)] + packed_outs
        scratch = []
        lines = pltpu.VMEM((CHUNKS // 2, FACE), jnp.int32)
        half_rows = CHUNKS // 2 * 8
        if first:
            chosen, own = call(
                select_into, [VM, VM], [f32(half_rows, FACE), f32(HALF, FACE)], "select", [lines]
            )(own, coarse_rows)
            outs = outs + [f32(half_rows, FACE)]
            scratch = [f32(HALF, FACE), lines]
            third = coarse_rows
        else:
            chosen, third = sel
        res = call(
            functools.partial(local_body, first),
            [VM, VM, VM, VM, VM, VM, SM],
            outs,
            "local",
            scratch,
        )(own, chosen, other, third, local, basis, table)
        if first:
            sel = (chosen, res[3])
        return (res[0], *exchange(*res[1:3])), sel

    base = [VM, VM, VM, SM, VM, VM]
    buf, far, loads, basis = call(
        pack_body,
        [LATE, LATE, SM, SM, SM],
        packed_outs + [f32(LOADS, ORDER), f32(CONS, ORDER)],
        "pack",
    )(*firsts)
    packed = (buf, far)
    done, sel = precondition(packed, loads, True, None, basis)
    step, residual, *packed = call(
        functools.partial(step_body, True),
        base,
        [f32(LOADS, ORDER), f32(LOADS, ORDER)] + packed_outs,
        "step",
    )(*done, table, loads, schur)
    done, sel = precondition(packed, residual, False, sel, basis)
    ends = [plain(LOADS, ORDER)] * 2
    return tuple(
        call(functools.partial(step_body, False), base + [VM], ends, "step")(
            *done, table, residual, schur, step
        )
    )


def solution(mesh):
    finer = Mesh(mesh.devices.reshape(NY, NZ // NV, NV, NX, NC), ALL)
    spec = P(ALL, None)
    return jax.shard_map(
        per_device, mesh=finer, in_specs=(spec,) * 9, out_specs=(spec, spec), check_vma=False
    )
```
